128 devices in a mesh: role: 4 (over y), section: 2 (over core), mp: 16 (over z, x).
Axes of the slice: x: 4, y: 4, z: 4, core: 2. Of those that a mesh axis runs over, the one named last changes fastest.
Arguments:
- states: bfloat16 [16, 64, 8192], P('role', None, 'mp'), may hold values from -6 to 6
- weights: bfloat16 [2, 8192, 8192], P('section', None, 'mp'), may hold values from -0.0625 to 0.0625
- head: bfloat16 [8192], P('mp'), may hold values from -0.0625 to 0.0625
- lengths: int32 [16], P('role'), may hold values from 1 to 64, as said below
- rewards: int32 [16], P('role'), may hold values from 0 to 1000
Outputs:
- weight_grads: bfloat16 [2, 8192, 8192], P('section', 'role', 'mp')
The draws below stay inside these ranges and needn't reach their ends.
Inputs may be any that keep to these rules, and one draw needn't show every extreme that they name: `lengths`: at least one dialogue fills all 64 slots.
All inputs are finite; a program needn't handle non-finite values.
Results may differ from the reference program's by a relative error of at most 0.014.
Values may be sent and summed in bfloat16 or wider, within the bound.
A program may use at most 192 MiB of HBM per device.

```python
import jax
import jax.numpy as jnp
from jax import lax

D = 8192
DLG = 4
LEN = 64
MB = 4
DIALOGS = 16
N_ROLE = 4
N_SECTION = 2
N_MP = 16


def draw_lengths(key, part):
    first_key, second_key = jax.random.split(jax.random.fold_in(key, 7))
    base = jax.random.randint(first_key, (DIALOGS,), 1, LEN + 1)
    chosen = jax.random.randint(second_key, (), 0, DIALOGS)
    return jnp.where(jnp.arange(DIALOGS) == chosen, LEN, base).astype(jnp.int32)


def with_ends(values, rng, least, top_value):
    longest = values.shape.index(max(values.shape))
    spots = []
    for shift in (0, 1):
        where = [jax.random.randint(jax.random.fold_in(rng, axis), (), 0, length) for axis, length in enumerate(values.shape)]
        where[longest] = (where[longest] + shift) % values.shape[longest]
        spots.append(tuple(where))
    return values.at[spots[0]].set(least).at[spots[1]].set(top_value)


def steps_of(own_key, extent, pieces, low, top_value):
    def one(dim, parts):
        heights = jax.random.uniform(jax.random.fold_in(jax.random.fold_in(own_key, 6), dim), (parts,), jnp.float32, low / len(pieces), top_value / len(pieces))
        return jnp.repeat(jnp.exp(heights), extent[dim] // parts).reshape((-1,) + (1,) * (len(extent) - dim - 1))

    gain = one(*pieces[0])
    for cut in pieces[1:]:
        gain = gain * one(*cut)
    return gain


def gaussian(own_key, dims, scale, limit, shards=(), kind=jnp.bfloat16):
    gain = steps_of(own_key, dims, shards, -0.22, 0.18) if shards else 1.0
    drawn = jax.random.normal(own_key, dims, jnp.float32) * scale * gain
    return jnp.minimum(jnp.maximum(drawn, -limit), limit).astype(kind)


def setup_inputs(seed: int = 0) -> dict:
    seeds = jax.random.split(jax.random.key(seed), 6)
    states = gaussian(seeds[0], (DIALOGS, LEN, D), 1.0, 6.0, ((0, 4), (2, 16)))
    weights = gaussian(seeds[1], (N_SECTION, D, D), D ** -0.5, 0.0625, ((0, 2), (2, 16)))
    head = gaussian(seeds[2], (D,), D ** -0.5, 0.0625, ((0, 16),))
    lengths = draw_lengths(jax.random.fold_in(seeds[5], 71), 0)
    rewards = with_ends(jax.random.randint(seeds[4], (DIALOGS,), 0, 1001), jax.random.fold_in(seeds[4], 1), 0, 1000).astype(jnp.int32)
    return {"states": states, "weights": weights, "head": head, "lengths": lengths, "rewards": rewards}


GAMMA = 0.97


def silu_slope(z):
    sig = jax.nn.sigmoid(z)
    return sig * (1.0 + z * (1.0 - sig))


def targets_of(lengths, rewards, span):
    places = jnp.arange(span, dtype=jnp.int32)[None, :]
    live = places < lengths[:, None]
    mask = live.astype(jnp.float32)
    power = jnp.where(live, lengths[:, None] - 1 - places, 0).astype(jnp.float32)
    target = rewards.astype(jnp.float32)[:, None] / 1000.0 * jnp.power(jnp.float32(GAMMA), power) * mask
    return target.astype(jnp.bfloat16), mask


def reference(states, weights, head, lengths, rewards):
    share = DLG // N_ROLE
    block_rows = DLG * LEN // MB
    width = D // N_MP
    head_f = head.astype(jnp.float32)
    first_w = weights[0]
    second_w = weights[1]
    grad_first = jnp.zeros((D, D), jnp.float32)
    grad_second = jnp.zeros((D, D), jnp.float32)
    for owner in range(N_ROLE):
        picks = jnp.concatenate([group * DLG + owner * share + jnp.arange(share, dtype=jnp.int32) for group in range(N_ROLE)]).astype(jnp.int32)
        rows = states[picks].reshape(DLG * LEN, D)
        target, mask = targets_of(lengths[picks], rewards[picks], LEN)
        target = lax.optimization_barrier(target).astype(jnp.float32).reshape(-1)
        mask = mask.reshape(-1)
        for micro in range(MB):
            lo_row = micro * block_rows
            x = rows[lo_row:lo_row + block_rows]
            goal = target[lo_row:lo_row + block_rows]
            keep = mask[lo_row:lo_row + block_rows]
            z0 = jnp.dot(x, first_w, preferred_element_type=jnp.float32)
            y1 = (x.astype(jnp.float32) + jax.nn.silu(z0)).astype(jnp.bfloat16)
            z1 = jnp.dot(y1, second_w, preferred_element_type=jnp.float32)
            y2 = (y1.astype(jnp.float32) + jax.nn.silu(z1)).astype(jnp.bfloat16)
            value = jnp.dot(y2, head, preferred_element_type=jnp.float32)
            err = (value - goal) * keep
            dy2 = err[:, None] * head_f[None, :]
            dz1 = (dy2 * silu_slope(z1)).astype(jnp.bfloat16)
            blocks = jnp.einsum("rjc,djc->jrd", dz1.astype(jnp.float32).reshape(block_rows, N_MP, width), second_w.astype(jnp.float32).reshape(D, N_MP, width))
            blocks = lax.optimization_barrier(blocks.astype(jnp.bfloat16)).astype(jnp.float32)
            back1 = jnp.sum(blocks, axis=0)
            dx1 = (dy2 + back1).astype(jnp.bfloat16)
            dz0 = (dx1.astype(jnp.float32) * silu_slope(z0)).astype(jnp.bfloat16)
            grad_second = grad_second + jnp.dot(y1.T, dz1, preferred_element_type=jnp.float32)
            grad_first = grad_first + jnp.dot(x.T, dz0, preferred_element_type=jnp.float32)
    return jnp.stack([grad_first, grad_second]).astype(jnp.bfloat16)
```

```python
import functools
import math

import jax
import jax.numpy as jnp
from jax import lax
from jax.experimental import pallas as pl
from jax.experimental.pallas import tpu as pltpu
from jax.sharding import PartitionSpec as P

MESH = pl.DeviceIdType.MESH
BF = jnp.bfloat16
F32 = jnp.float32
GAMMA = 0.97

N = 4
ROWS = 256
HALF = 128
QUART = 64
W = 512
NSEM = 200
HALVES = ((0, "x", "z"), (HALF, "z", "x"))
SIGNS = (1, -1)


def sigmoid(v):
    return 1.0 / (1.0 + jnp.exp(-v))


def kernel(states, weight, head_ref, lengths, rewards, out, wv, gath, across, relay, acc, slope,
           part, r1, r2, r3, r4, sums, dz, dzt, y1, err, vx, vz, gacc, gout,
           send_sem, recv_sem, local_sem):
    role = lax.axis_index("role")
    section = lax.axis_index("section")
    mp = lax.axis_index("mp")
    pos = {"z": mp // N, "x": mp % N}
    me = {"role": role, "section": section, "mp": mp}

    def slot(**off):
        z = lax.rem(pos["z"] + off.get("z", 0) % N, N)
        x = lax.rem(pos["x"] + off.get("x", 0) % N, N)
        return z * N + x

    def role_at(off):
        return lax.rem(role + off % N, N)

    def device(mp_index=None, role_index=None, sec=None):
        return (
            role if role_index is None else role_index,
            section if sec is None else sec,
            mp if mp_index is None else mp_index,
        )

    numbers = {}

    def number(key):
        return numbers.setdefault(key, len(numbers))

    def move(key, src, dst, dev):
        i = number(key)
        assert i < NSEM
        return pltpu.make_async_remote_copy(
            src_ref=src, dst_ref=dst, send_sem=send_sem.at[i], recv_sem=recv_sem.at[i],
            device_id=dev, device_id_type=MESH,
        )

    started = []

    def send(key, src, dst, dev):
        copy = move(key, src, dst, dev)
        copy.start()
        started.append(copy)

    def arrive(key, dst):
        move(key, dst, dst, device(mp_index=slot(x=1))).wait_recv()

    def drain():
        for copy in started:
            copy.wait_send()
        started.clear()

    def rows_of(base, sign):
        return pl.ds(base + (0 if sign > 0 else QUART), QUART)

    def gather_first(src, sec, halves=(0, 1)):
        for h in halves:
            base, f, g = HALVES[h]
            rows = pl.ds(base, HALF)
            for axis, kind in ((f, "f"), (g, "g")):
                for sg in SIGNS:
                    key = ("f", sec, h, sg) if kind == "f" else ("g", sec, h, sg, 0)
                    send(key, src.at[rows], gath.at[mp, rows], device(slot(**{axis: sg}), sec=sec))

    def gather_rest(sec, use):
        def region(h, df, dg, rows):
            _, f, g = HALVES[h]
            return gath.at[slot(**{f: df, g: dg}), rows]

        def forward(key, ref, axis, sg):
            send(key, ref, ref, device(slot(**{axis: sg})))

        for sg in SIGNS:
            for h, (base, f, g) in enumerate(HALVES):
                rows = pl.ds(base, HALF)
                block = region(h, -sg, 0, rows)
                arrive(("f", sec, h, sg), block)
                forward(("o", sec, h, sg), region(h, -sg, 0, rows_of(base, sg)), f, sg)
                for s2 in SIGNS:
                    forward(("g", sec, h, s2, sg), block, g, s2)
        for sg in SIGNS:
            for h, (base, f, g) in enumerate(HALVES):
                rows = pl.ds(base, HALF)
                arrive(("g", sec, h, sg, 0), region(h, 0, -sg, rows))
                forward(("t", sec, h, sg, 0), region(h, 0, -sg, rows_of(base, sg)), g, sg)
        for sg in SIGNS:
            for h, (base, f, g) in enumerate(HALVES):
                block = region(h, 2, 0, rows_of(base, sg))
                arrive(("o", sec, h, sg), block)
                for s2 in SIGNS:
                    forward(("g", sec, h, s2, 2 * sg), block, g, s2)
        use([(0, 0), (0, 1), (0, -1), (1, 0), (-1, 0)])
        for sf in SIGNS:
            for sg in SIGNS:
                for h, (base, f, g) in enumerate(HALVES):
                    arrive(("g", sec, h, sg, sf), region(h, -sf, -sg, pl.ds(base, HALF)))
                    forward(("t", sec, h, sg, sf), region(h, -sf, -sg, rows_of(base, sg)), g, sg)
        for sg in SIGNS:
            for h, (base, f, g) in enumerate(HALVES):
                arrive(("g", sec, h, sg, 2 * sg), region(h, 2, -sg, rows_of(base, sg)))
                forward(("t", sec, h, sg, 2), region(h, 2, -sg, rows_of(base, sg)), g, sg)
        use([(1, 1), (1, -1), (-1, 1), (-1, -1)])
        for sg in SIGNS:
            for h, (base, f, g) in enumerate(HALVES):
                arrive(("g", sec, h, sg, -2 * sg), region(h, 2, -sg, rows_of(base, -sg)))
                arrive(("t", sec, h, sg, 0), region(h, 0, 2, rows_of(base, sg)))
        use([(2, 0), (0, 2)])
        for sf in SIGNS:
            for sg in SIGNS:
                for h, (base, f, g) in enumerate(HALVES):
                    arrive(("t", sec, h, sg, sf), region(h, -sf, 2, rows_of(base, sg)))
        use([(1, 2), (-1, 2), (2, 1), (2, -1)])
        for sg in SIGNS:
            for h, (base, f, g) in enumerate(HALVES):
                arrive(("t", sec, h, sg, 2), region(h, 2, 2, rows_of(base, sg)))
        use([(2, 2)])

    def project(offsets):
        for dz_, dx_ in offsets:
            s = slot(z=dz_, x=dx_)
            add = jnp.dot(gath[s], wv[s], preferred_element_type=F32)
            if (dz_, dx_) == (0, 0):
                acc[...] = add
            else:
                acc[...] += add

    def across_first():
        for sg in SIGNS:
            far = role_at(2)
            rows = pl.ds(0 if sg > 0 else HALF, HALF)
            send(("br", sg), gath.at[pl.ds(far * N, N), rows], relay.at[0 if sg > 0 else 1],
                 device(role_index=role_at(sg)))
        for sg in SIGNS:
            to = role_at(sg)
            send(("b", sg), gath.at[pl.ds(to * N, N)], across.at[role], device(role_index=to))

    def across_relay():
        for sg in SIGNS:
            rows = pl.ds(0 if sg > 0 else HALF, HALF)
            block = relay.at[0 if sg > 0 else 1]
            arrive(("br", sg), block)
            send(("bf", sg), block, across.at[role_at(-sg), pl.ds(0, N), rows],
                 device(role_index=role_at(sg)))

    def across_last():
        for sg in SIGNS:
            arrive(("b", sg), across.at[role_at(-sg)])
        for sg in SIGNS:
            rows = pl.ds(0 if sg > 0 else HALF, HALF)
            arrive(("bf", sg), across.at[role_at(2), pl.ds(0, N), rows])

    def spread_first(src, sec, h):
        rows = pl.ds(h * HALF, HALF)
        order = (1, -1) if h == 0 else (-1, 1)
        for off in order:
            send(("d", sec, h, off), src.at[rows], dz.at[role, rows],
                 device(role_index=role_at(off), sec=sec))

    def spread_relay(sec):
        for h, sg in ((0, 1), (1, -1)):
            rows = pl.ds(h * HALF, HALF)
            block = dz.at[role_at(-sg), rows]
            arrive(("d", sec, h, sg), block)
            send(("do", sec, h), block, block, device(role_index=role_at(sg)))

    def spread_near(sec):
        for h, sg in ((0, -1), (1, 1)):
            arrive(("d", sec, h, sg), dz.at[role_at(-sg), pl.ds(h * HALF, HALF)])

    def spread_far(sec):
        for h in (0, 1):
            arrive(("do", sec, h), dz.at[role_at(2), pl.ds(h * HALF, HALF)])

    tn = (((0,), (0,)), ((), ()))

    def grads(off):
        src = role_at(off)
        for j in range(N):
            left = gath[role * N + j] if off == 0 else across[src, j]
            add = lax.dot_general(left, dz[src], tn, preferred_element_type=F32)
            if off == 0:
                gacc[j] = add
            elif off == 2:
                gout[j] = (gacc[j] + add).astype(BF)
                pltpu.make_async_copy(gout.at[j], out.at[j], local_sem.at[2 + j]).start()
            else:
                gacc[j] += add

    def grads_done():
        for j in range(N):
            pltpu.make_async_copy(gout.at[j], out.at[j], local_sem.at[2 + j]).wait()

    def by_rows(base, count, body, step=32):
        @pl.loop(0, count // step)
        def _(i):
            body(pl.ds(pl.multiple_of(base + i * step, step), step))

    load_w = pltpu.make_async_copy(weight, wv, local_sem.at[0])
    load_w.start()
    own_copy = pltpu.make_async_copy(states, gath.at[mp], local_sem.at[1])

    @pl.when(section == 0)
    def _():
        own_copy.start()

    barrier = pltpu.get_barrier_semaphore()
    peers = [device(sec=1 - section)]
    for sec in (section, 1 - section):
        peers += [device(slot(**{a: o}), sec=sec) for a in ("x", "z") for o in (1, 2, 3)]
        peers += [device(role_index=role_at(o), sec=sec) for o in (1, 2, 3)]
    for dev in peers:
        pl.semaphore_signal(barrier, inc=1, device_id=dev, device_id_type=MESH)
    pl.semaphore_wait(barrier, len(peers))

    @pl.when(section == 0)
    def _():
        gather_first(states, 0)
        own_copy.wait()
        load_w.wait()
        gather_rest(0, project)
        across_first()
        for h in (0, 1):
            def first_layer(rows):
                z = acc[rows]
                y1[rows] = (gath[mp, rows].astype(F32) + z * sigmoid(z)).astype(BF)
            by_rows(h * HALF, HALF, first_layer)
            gather_first(y1, 1, (h,))
        send(("own",), y1, gath.at[mp], device(sec=1))

        def first_slope(rows):
            z = acc[rows]
            s = sigmoid(z)
            acc[rows] = s * (1.0 + z * (1.0 - s))
        by_rows(0, ROWS, first_slope)
        send(("slope",), acc, slope, device(sec=1))
        across_relay()
        across_last()
        for h in (0, 1):
            arrive(("down", h), dz.at[role, pl.ds(h * HALF, HALF)])
        spread_relay(0)
        grads(0)
        spread_near(0)
        grads(1)
        grads(-1)
        spread_far(0)
        grads(2)
        grads_done()
        drain()

    @pl.when(section == 1)
    def _():
        load_w.wait()

        def use(offsets):
            if (0, 0) in offsets:
                arrive(("own",), gath.at[mp])
            project(offsets)

        gather_rest(1, use)
        across_first()

        head = head_ref[...]
        head_f = head.astype(F32)

        def second_layer(rows):
            z = acc[rows]
            s = sigmoid(z)
            y1[rows] = (gath[mp, rows].astype(F32) + z * s).astype(BF)
            g = head_f * (s * (1.0 + z * (1.0 - s)))
            acc[rows] = g
            dzt[rows] = g.astype(BF)
        by_rows(0, ROWS, second_layer)

        nt = (((1,), (1,)), ((), ()))
        vx[0] = lax.dot_general(jnp.broadcast_to(head, (16, W)), y1[...], nt,
                                preferred_element_type=F32)[:8]
        for o in (1, 2, 3):
            send(("vx", o), vx.at[0], vx.at[o], device(slot(x=o)))

        made = set()

        def make(z_off, x_off):
            z_off, x_off = z_off % N, x_off % N
            if (z_off, x_off) in made:
                return
            made.add((z_off, x_off))
            s = slot(z=z_off, x=x_off)
            part[s] = lax.dot_general(dzt[...], wv[s], nt, preferred_element_type=F32).astype(BF)

        def make_at(h, df, dg):
            _, f, g = HALVES[h]
            off = {f: df, g: dg}
            make(off["z"], off["x"])
            return slot(**off)

        order = (2, 1, 3, 0)
        for dg in order:
            for h, (base, f, g) in enumerate(HALVES):
                s = make_at(h, 2, dg)
                for k, sg in enumerate(SIGNS):
                    send(("r1", h, sg, dg), part.at[s, rows_of(base, sg)], r1.at[h, k, dg],
                         device(slot(**{f: sg})))
        for o in (1, 2, 3):
            arrive(("vx", o), vx.at[o])
        vz[0] = (vx[0] + vx[1]) + (vx[2] + vx[3])
        for o in (1, 2, 3):
            send(("vz", o), vz.at[0], vz.at[o], device(slot(z=o)))
        for dg in order:
            for h, (base, f, g) in enumerate(HALVES):
                for k, sg in enumerate(SIGNS):
                    s = make_at(h, sg, dg)
                    arrive(("r1", h, sg, dg), r1.at[h, k, dg])
                    rows = rows_of(base, sg)
                    part[s, rows] = (part[s, rows].astype(F32) + r1[h, k, dg].astype(F32)).astype(BF)
                    send(("r2", h, sg, dg), part.at[s, pl.ds(base, HALF)], r2.at[h, k, dg],
                         device(slot(**{f: sg})))
        make(0, 0)

        for o in (1, 2, 3):
            arrive(("vz", o), vz.at[o])
        value = (vz[0] + vz[1]) + (vz[2] + vz[3])
        lane = lax.broadcasted_iota(jnp.int32, (8, ROWS), 1)
        count = lengths.shape[0]
        span = ROWS // count
        place, which = lane % span, lane // span
        length = jnp.full((8, ROWS), lengths[0], jnp.int32)
        reward = jnp.full((8, ROWS), rewards[0], jnp.int32)
        for d in range(1, count):
            length = jnp.where(which == d, lengths[d], length)
            reward = jnp.where(which == d, rewards[d], reward)
        live = place < length
        mask = live.astype(F32)
        power = jnp.where(live, length - 1 - place, 0).astype(F32)
        target = reward.astype(F32) / 1000.0 * jnp.exp(power * math.log(GAMMA)) * mask
        error = (value - target.astype(BF).astype(F32)) * mask
        err[...] = jnp.broadcast_to(error[0:1], (128, ROWS)).T

        def second_grad(rows):
            dz[role, rows] = (err[rows][:, 0:1] * acc[rows]).astype(BF)
        by_rows(0, ROWS, second_grad)
        for h in (0, 1):
            spread_first(dz.at[role], 1, h)

        for dg in order:
            for h, (base, f, g) in enumerate(HALVES):
                s = slot(**{f: 0, g: dg})
                rows = pl.ds(base, HALF)
                for k, sg in enumerate(SIGNS):
                    arrive(("r2", h, sg, dg), r2.at[h, k, dg])
                total = part[s, rows].astype(F32) + r2[h, 0, dg].astype(F32) + r2[h, 1, dg].astype(F32)
                sums[h, dg] = total.astype(BF)
                if dg == 2:
                    for k, sg in enumerate(SIGNS):
                        send(("r3", h, sg), sums.at[h, dg, rows_of(0, sg)], r3.at[h, k],
                             device(slot(**{g: sg})))
                elif dg in (1, 3):
                    sg = 1 if dg == 1 else -1
                    k = SIGNS.index(sg)
                    arrive(("r3", h, sg), r3.at[h, k])
                    rows = rows_of(0, sg)
                    sums[h, dg, rows] = (sums[h, dg, rows].astype(F32) + r3[h, k].astype(F32)).astype(BF)
                    send(("r4", h, sg), sums.at[h, dg], r4.at[h, k], device(slot(**{g: sg})))
        arrive(("slope",), slope)
        for h, (base, f, g) in enumerate(HALVES):
            for k, sg in enumerate(SIGNS):
                arrive(("r4", h, sg), r4.at[h, k])

            @pl.loop(0, HALF // 32)
            def _(i):
                low = pl.ds(pl.multiple_of(i * 32, 32), 32)
                rows = pl.ds(pl.multiple_of(base + i * 32, 32), 32)
                back = sums[h, 0, low].astype(F32) + r4[h, 0, low].astype(F32) + r4[h, 1, low].astype(F32)
                e = err[rows][:, 0:1]
                dx = (e * head_f + e * back).astype(BF).astype(F32)
                dzt[rows] = (dx * slope[rows]).astype(BF)
            send(("down", h), dzt.at[pl.ds(base, HALF)], dz.at[role, pl.ds(base, HALF)], device(sec=0))
            spread_first(dzt, 0, h)
        across_relay()
        across_last()
        spread_relay(1)
        spread_near(1)
        spread_far(1)
        grads(0)
        grads(1)
        grads(-1)
        grads(2)
        grads_done()
        drain()


def per_device(states, weights, head, lengths, rewards):
    dialogs, span, width = states.shape
    rows = dialogs * span
    deep = weights.shape[1]
    blocks = deep // width
    dma = pltpu.SemaphoreType.DMA
    vmem = pltpu.VMEM
    out = pl.pallas_call(
        kernel,
        out_shape=jax.ShapeDtypeStruct((N, width, width), BF),
        in_specs=[
            pl.BlockSpec(memory_space=pl.ANY),
            pl.BlockSpec(memory_space=pl.ANY),
            pl.BlockSpec(memory_space=pltpu.VMEM),
            pl.BlockSpec(memory_space=pltpu.SMEM),
            pl.BlockSpec(memory_space=pltpu.SMEM),
        ],
        out_specs=pl.BlockSpec(memory_space=pl.ANY),
        scratch_shapes=[
            vmem((blocks, width, width), BF),
            vmem((blocks, rows, width), BF),
            vmem((N, N, rows, width), BF),
            vmem((2, N, HALF, width), BF),
            vmem((rows, width), F32),
            vmem((rows, width), F32),
            vmem((blocks, rows, width), BF),
            vmem((2, 2, N, QUART, width), BF),
            vmem((2, 2, N, HALF, width), BF),
            vmem((2, 2, QUART, width), BF),
            vmem((2, 2, HALF, width), BF),
            vmem((2, N, HALF, width), BF),
            vmem((N, rows, width), BF),
            vmem((rows, width), BF),
            vmem((rows, width), BF),
            vmem((rows, 128), F32),
            vmem((N, 8, rows), F32),
            vmem((N, 8, rows), F32),
            vmem((N, width, width), F32),
            vmem((N, width, width), BF),
            dma((NSEM,)),
            dma((NSEM,)),
            dma((8,)),
        ],
        compiler_params=pltpu.CompilerParams(
            collective_id=0, has_side_effects=True, vmem_limit_bytes=60 * 1024 * 1024,
        ),
        name="window_grad",
    )(
        states.reshape(rows, width),
        weights.reshape(blocks, width, width),
        head.reshape(1, width),
        lengths,
        rewards,
    )
    return out.reshape(1, N * width, width)


def solution(mesh):
    placed = (P("role", None, "mp"), P("section", None, "mp"), P("mp"), P("role"), P("role"))
    return jax.shard_map(
        per_device,
        mesh=mesh,
        in_specs=placed,
        out_specs=P("section", "role", "mp"),
        check_vma=False,
    )
```

```python
import functools
import math

import jax
import jax.numpy as jnp
from jax import lax
from jax.experimental import pallas as pl
from jax.experimental.pallas import tpu as pltpu
from jax.sharding import PartitionSpec as P

MESH = pl.DeviceIdType.MESH
BF = jnp.bfloat16
F32 = jnp.float32
GAMMA = 0.97

N = 4
ROWS = 256
HALF = 128
QUART = 64
W = 512
NSEM = 200
HALVES = ((0, "x", "z"), (HALF, "z", "x"))
SIGNS = (1, -1)


def sigmoid(v):
    return 1.0 / (1.0 + jnp.exp(-v))


def kernel(states, weight, head_ref, lengths, rewards, out, wv, gath, across, relay, acc, slope,
           part, r1, r2, r3, r4, sums, dz, dzt, y1, err, vx, vz, gacc, gout,
           send_sem, recv_sem, far_send, far_recv, pair_send, pair_recv, local_sem):
    role = lax.axis_index("role")
    section = lax.axis_index("section")
    mp = lax.axis_index("mp")
    pos = {"z": mp // N, "x": mp % N}
    me = {"role": role, "section": section, "mp": mp}

    def slot(**off):
        z = lax.rem(pos["z"] + off.get("z", 0) % N, N)
        x = lax.rem(pos["x"] + off.get("x", 0) % N, N)
        return z * N + x

    def role_at(off):
        return lax.rem(role + off % N, N)

    def device(mp_index=None, role_index=None, sec=None):
        return (
            role if role_index is None else role_index,
            section if sec is None else sec,
            mp if mp_index is None else mp_index,
        )

    numbers = {}

    def number(key):
        return numbers.setdefault(key, len(numbers))

    def move(key, src, dst, dev):
        i = number(key)
        assert i < NSEM
        return pltpu.make_async_remote_copy(
            src_ref=src, dst_ref=dst, send_sem=send_sem.at[i], recv_sem=recv_sem.at[i],
            device_id=dev, device_id_type=MESH,
        )

    started = []

    def send(key, src, dst, dev):
        copy = move(key, src, dst, dev)
        copy.start()
        started.append(copy)

    def arrive(key, dst):
        move(key, dst, dst, device(mp_index=slot(x=1))).wait_recv()

    def drain():
        for copy in started:
            copy.wait_send()
        started.clear()

    def rows_of(base, sign):
        return pl.ds(base + (0 if sign > 0 else QUART), QUART)

    def gather_first(src, sec, halves=(0, 1)):
        for h in halves:
            base, f, g = HALVES[h]
            rows = pl.ds(base, HALF)
            for axis, kind in ((f, "f"), (g, "g")):
                for sg in SIGNS:
                    key = ("f", sec, h, sg) if kind == "f" else ("g", sec, h, sg, 0)
                    send(key, src.at[rows], gath.at[mp, rows], device(slot(**{axis: sg}), sec=sec))

    def gather_rest(sec, use):
        def region(h, df, dg, rows):
            _, f, g = HALVES[h]
            return gath.at[slot(**{f: df, g: dg}), rows]

        def forward(key, ref, axis, sg):
            send(key, ref, ref, device(slot(**{axis: sg})))

        for sg in SIGNS:
            for h, (base, f, g) in enumerate(HALVES):
                rows = pl.ds(base, HALF)
                block = region(h, -sg, 0, rows)
                arrive(("f", sec, h, sg), block)
                forward(("o", sec, h, sg), region(h, -sg, 0, rows_of(base, sg)), f, sg)
                for s2 in SIGNS:
                    forward(("g", sec, h, s2, sg), block, g, s2)
        for sg in SIGNS:
            for h, (base, f, g) in enumerate(HALVES):
                rows = pl.ds(base, HALF)
                arrive(("g", sec, h, sg, 0), region(h, 0, -sg, rows))
                forward(("t", sec, h, sg, 0), region(h, 0, -sg, rows_of(base, sg)), g, sg)
        for sg in SIGNS:
            for h, (base, f, g) in enumerate(HALVES):
                block = region(h, 2, 0, rows_of(base, sg))
                arrive(("o", sec, h, sg), block)
                for s2 in SIGNS:
                    forward(("g", sec, h, s2, 2 * sg), block, g, s2)
        use([(0, 0), (0, 1), (0, -1), (1, 0), (-1, 0)])
        for sf in SIGNS:
            for sg in SIGNS:
                for h, (base, f, g) in enumerate(HALVES):
                    arrive(("g", sec, h, sg, sf), region(h, -sf, -sg, pl.ds(base, HALF)))
                    forward(("t", sec, h, sg, sf), region(h, -sf, -sg, rows_of(base, sg)), g, sg)
        for sg in SIGNS:
            for h, (base, f, g) in enumerate(HALVES):
                arrive(("g", sec, h, sg, 2 * sg), region(h, 2, -sg, rows_of(base, sg)))
                forward(("t", sec, h, sg, 2), region(h, 2, -sg, rows_of(base, sg)), g, sg)
        use([(1, 1), (1, -1), (-1, 1), (-1, -1)])
        for sg in SIGNS:
            for h, (base, f, g) in enumerate(HALVES):
                arrive(("g", sec, h, sg, -2 * sg), region(h, 2, -sg, rows_of(base, -sg)))
                arrive(("t", sec, h, sg, 0), region(h, 0, 2, rows_of(base, sg)))
        use([(2, 0), (0, 2)])
        for sf in SIGNS:
            for sg in SIGNS:
                for h, (base, f, g) in enumerate(HALVES):
                    arrive(("t", sec, h, sg, sf), region(h, -sf, 2, rows_of(base, sg)))
        use([(1, 2), (-1, 2), (2, 1), (2, -1)])
        for sg in SIGNS:
            for h, (base, f, g) in enumerate(HALVES):
                arrive(("t", sec, h, sg, 2), region(h, 2, 2, rows_of(base, sg)))
        use([(2, 2)])

    def project(offsets, far=True):
        across_send(offsets, far)
        for dz_, dx_ in offsets:
            s = slot(z=dz_, x=dx_)
            add = jnp.dot(gath[s], wv[s], preferred_element_type=F32)
            if (dz_, dx_) == (0, 0):
                acc[...] = add
            else:
                acc[...] += add

    def across_send(offsets, far):
        for z_off, x_off in offsets:
            s = slot(z=z_off, x=x_off)
            to = s // N

            @pl.when(to != role if far else lax.rem(to + role, 2) == 1)
            def _():
                pltpu.make_async_remote_copy(
                    src_ref=gath.at[s], dst_ref=across.at[role, lax.rem(s, N)],
                    send_sem=far_send.at[s], recv_sem=far_recv.at[role * N + lax.rem(s, N)],
                    device_id=device(role_index=to), device_id_type=MESH,
                ).start()

    def across_wait(off, wait):
        other = role_at(off)
        for j in range(N):
            copy = pltpu.make_async_remote_copy(
                src_ref=across.at[other, j], dst_ref=across.at[other, j],
                send_sem=far_send.at[other * N + j], recv_sem=far_recv.at[other * N + j],
                device_id=device(role_index=role_at(1)), device_id_type=MESH,
            )
            copy.wait_recv() if wait == "recv" else copy.wait_send()

    line = (("x", pos["x"]), ("z", pos["z"]))

    def pair_first():
        far = role_at(2)
        for h, (axis, at) in enumerate(line):
            send(("pair", h), gath.at[far * N + at, pl.ds(h * HALF, HALF)], relay.at[h],
                 device(role_index=far, sec=0))

    def pair_relay():
        for h, (axis, at) in enumerate(line):
            arrive(("pair", h), relay.at[h])
            for off in (2, 1, 3, 0):
                copy = pltpu.make_async_remote_copy(
                    src_ref=relay.at[h], dst_ref=across.at[role_at(2), at, pl.ds(h * HALF, HALF)],
                    send_sem=pair_send.at[h, off], recv_sem=pair_recv.at[h, at],
                    device_id=device(slot(**{axis: off}), sec=1), device_id_type=MESH,
                )
                copy.start()
                started.append(copy)

    def pair_wait():
        for h in (0, 1):
            for j in range(N):
                block = across.at[role_at(2), j, pl.ds(h * HALF, HALF)]
                pltpu.make_async_remote_copy(
                    src_ref=block, dst_ref=block, send_sem=pair_send.at[h, j], recv_sem=pair_recv.at[h, j],
                    device_id=device(sec=0), device_id_type=MESH,
                ).wait_recv()

    def spread_first(src, sec, h):
        rows = pl.ds(h * HALF, HALF)
        for off in (2, 1, 3):
            send(("d", sec, h, off), src.at[rows], dz.at[role, rows],
                 device(role_index=role_at(off), sec=sec))

    def spread_wait(sec, off):
        for h in (0, 1):
            arrive(("d", sec, h, -off % N), dz.at[role_at(off), pl.ds(h * HALF, HALF)])

    tn = (((0,), (0,)), ((), ()))

    def grads(off):
        src = role_at(off)
        for j in range(N):
            left = gath[role * N + j] if off == 0 else across[src, j]
            add = lax.dot_general(left, dz[src], tn, preferred_element_type=F32)
            if off == 0:
                gacc[j] = add
            elif off == 2:
                gout[j] = (gacc[j] + add).astype(BF)
                pltpu.make_async_copy(gout.at[j], out.at[j], local_sem.at[2 + j]).start()
            else:
                gacc[j] += add

    def grads_done():
        for j in range(N):
            pltpu.make_async_copy(gout.at[j], out.at[j], local_sem.at[2 + j]).wait()

    def by_rows(base, count, body, step=32):
        @pl.loop(0, count // step)
        def _(i):
            body(pl.ds(pl.multiple_of(base + i * step, step), step))

    load_w = pltpu.make_async_copy(weight, wv, local_sem.at[0])
    load_w.start()
    own_copy = pltpu.make_async_copy(states, gath.at[mp], local_sem.at[1])

    @pl.when(section == 0)
    def _():
        own_copy.start()

    barrier = pltpu.get_barrier_semaphore()
    peers = [device(sec=1 - section)]
    for sec in (section, 1 - section):
        peers += [device(slot(**{a: o}), sec=sec) for a in ("x", "z") for o in (1, 2, 3)]
        peers += [device(role_index=role_at(o), sec=sec) for o in (1, 2, 3)]
    for dev in peers:
        pl.semaphore_signal(barrier, inc=1, device_id=dev, device_id_type=MESH)
    pl.semaphore_wait(barrier, len(peers))

    @pl.when(section == 0)
    def _():
        gather_first(states, 0)
        own_copy.wait()
        load_w.wait()
        gather_rest(0, project)
        for h in (0, 1):
            def first_layer(rows):
                z = acc[rows]
                y1[rows] = (gath[mp, rows].astype(F32) + z * sigmoid(z)).astype(BF)
            by_rows(h * HALF, HALF, first_layer)
            gather_first(y1, 1, (h,))
        send(("own",), y1, gath.at[mp], device(sec=1))

        def first_slope(rows):
            z = acc[rows]
            s = sigmoid(z)
            acc[rows] = s * (1.0 + z * (1.0 - s))
        by_rows(0, ROWS, first_slope)
        send(("slope",), acc, slope, device(sec=1))
        pair_relay()
        for h in (0, 1):
            arrive(("down", h), dz.at[role, pl.ds(h * HALF, HALF)])
        grads(0)
        for off in (1, 3, 2):
            spread_wait(0, off)
            across_wait(off, "recv")
            grads(off)
        grads_done()
        for off in (1, 2, 3):
            across_wait(off, "send")
        drain()

    @pl.when(section == 1)
    def _():
        load_w.wait()

        def use(offsets):
            if (0, 0) in offsets:
                arrive(("own",), gath.at[mp])
            project(offsets, far=False)

        gather_rest(1, use)
        pair_first()

        head = head_ref[...].reshape(1, W)
        head_f = head.astype(F32)

        def second_layer(rows):
            z = acc[rows]
            s = sigmoid(z)
            y1[rows] = (gath[mp, rows].astype(F32) + z * s).astype(BF)
            g = head_f * (s * (1.0 + z * (1.0 - s)))
            acc[rows] = g
            dzt[rows] = g.astype(BF)
        by_rows(0, ROWS, second_layer)

        nt = (((1,), (1,)), ((), ()))
        vx[0] = lax.dot_general(jnp.broadcast_to(head, (16, W)), y1[...], nt,
                                preferred_element_type=F32)[:8]
        for o in (1, 2, 3):
            send(("vx", o), vx.at[0], vx.at[o], device(slot(x=o)))

        made = set()

        def make(z_off, x_off):
            z_off, x_off = z_off % N, x_off % N
            if (z_off, x_off) in made:
                return
            made.add((z_off, x_off))
            s = slot(z=z_off, x=x_off)
            part[s] = lax.dot_general(dzt[...], wv[s], nt, preferred_element_type=F32).astype(BF)

        def make_at(h, df, dg):
            _, f, g = HALVES[h]
            off = {f: df, g: dg}
            make(off["z"], off["x"])
            return slot(**off)

        order = (2, 1, 3, 0)
        for dg in order:
            for h, (base, f, g) in enumerate(HALVES):
                s = make_at(h, 2, dg)
                for k, sg in enumerate(SIGNS):
                    send(("r1", h, sg, dg), part.at[s, rows_of(base, sg)], r1.at[h, k, dg],
                         device(slot(**{f: sg})))
        for o in (1, 2, 3):
            arrive(("vx", o), vx.at[o])
        vz[0] = (vx[0] + vx[1]) + (vx[2] + vx[3])
        for o in (1, 2, 3):
            send(("vz", o), vz.at[0], vz.at[o], device(slot(z=o)))
        for dg in order:
            for h, (base, f, g) in enumerate(HALVES):
                for k, sg in enumerate(SIGNS):
                    s = make_at(h, sg, dg)
                    arrive(("r1", h, sg, dg), r1.at[h, k, dg])
                    rows = rows_of(base, sg)
                    part[s, rows] = (part[s, rows].astype(F32) + r1[h, k, dg].astype(F32)).astype(BF)
                    send(("r2", h, sg, dg), part.at[s, pl.ds(base, HALF)], r2.at[h, k, dg],
                         device(slot(**{f: sg})))
        make(0, 0)

        for o in (1, 2, 3):
            arrive(("vz", o), vz.at[o])
        value = (vz[0] + vz[1]) + (vz[2] + vz[3])
        lane = lax.broadcasted_iota(jnp.int32, (8, ROWS), 1)
        count = lengths.shape[0]
        span = ROWS // count
        place, which = lane % span, lane // span
        length = jnp.full((8, ROWS), lengths[0], jnp.int32)
        reward = jnp.full((8, ROWS), rewards[0], jnp.int32)
        for d in range(1, count):
            length = jnp.where(which == d, lengths[d], length)
            reward = jnp.where(which == d, rewards[d], reward)
        live = place < length
        mask = live.astype(F32)
        power = jnp.where(live, length - 1 - place, 0).astype(F32)
        target = reward.astype(F32) / 1000.0 * jnp.exp(power * math.log(GAMMA)) * mask
        error = (value - target.astype(BF).astype(F32)) * mask
        err[...] = jnp.broadcast_to(error[0:1], (128, ROWS)).T

        def second_grad(rows):
            dz[role, rows] = (err[rows][:, 0:1] * acc[rows]).astype(BF)
        by_rows(0, ROWS, second_grad)
        for h in (0, 1):
            spread_first(dz.at[role], 1, h)

        for dg in order:
            for h, (base, f, g) in enumerate(HALVES):
                s = slot(**{f: 0, g: dg})
                rows = pl.ds(base, HALF)
                for k, sg in enumerate(SIGNS):
                    arrive(("r2", h, sg, dg), r2.at[h, k, dg])
                total = part[s, rows].astype(F32) + r2[h, 0, dg].astype(F32) + r2[h, 1, dg].astype(F32)
                sums[h, dg] = total.astype(BF)
                if dg == 2:
                    for k, sg in enumerate(SIGNS):
                        send(("r3", h, sg), sums.at[h, dg, rows_of(0, sg)], r3.at[h, k],
                             device(slot(**{g: sg})))
                elif dg in (1, 3):
                    sg = 1 if dg == 1 else -1
                    k = SIGNS.index(sg)
                    arrive(("r3", h, sg), r3.at[h, k])
                    rows = rows_of(0, sg)
                    sums[h, dg, rows] = (sums[h, dg, rows].astype(F32) + r3[h, k].astype(F32)).astype(BF)
                    send(("r4", h, sg), sums.at[h, dg], r4.at[h, k], device(slot(**{g: sg})))
        arrive(("slope",), slope)
        for h, (base, f, g) in enumerate(HALVES):
            for k, sg in enumerate(SIGNS):
                arrive(("r4", h, sg), r4.at[h, k])

            @pl.loop(0, HALF // 32)
            def _(i):
                low = pl.ds(pl.multiple_of(i * 32, 32), 32)
                rows = pl.ds(pl.multiple_of(base + i * 32, 32), 32)
                back = sums[h, 0, low].astype(F32) + r4[h, 0, low].astype(F32) + r4[h, 1, low].astype(F32)
                e = err[rows][:, 0:1]
                dx = (e * head_f + e * back).astype(BF).astype(F32)
                dzt[rows] = (dx * slope[rows]).astype(BF)
            send(("down", h), dzt.at[pl.ds(base, HALF)], dz.at[role, pl.ds(base, HALF)], device(sec=0))
            spread_first(dzt, 0, h)
        grads(0)
        for off in (1, 3, 2):
            spread_wait(1, off)
            if off == 2:
                pair_wait()
            else:
                across_wait(off, "recv")
            grads(off)
        grads_done()
        for off in (1, 3):
            across_wait(off, "send")
        drain()


def per_device(states, weights, head, lengths, rewards):
    dialogs, span, width = states.shape
    rows = dialogs * span
    deep = weights.shape[1]
    blocks = deep // width
    dma = pltpu.SemaphoreType.DMA
    vmem = pltpu.VMEM
    out = pl.pallas_call(
        kernel,
        out_shape=jax.ShapeDtypeStruct((N, width, width), BF),
        in_specs=[
            pl.BlockSpec(memory_space=pltpu.HBM),
            pl.BlockSpec(memory_space=pltpu.HBM),
            pl.BlockSpec(memory_space=pltpu.VMEM),
            pl.BlockSpec(memory_space=pltpu.SMEM),
            pl.BlockSpec(memory_space=pltpu.SMEM),
        ],
        out_specs=pl.BlockSpec(memory_space=pl.ANY),
        scratch_shapes=[
            vmem((blocks, width, width), BF),
            vmem((blocks, rows, width), BF),
            vmem((N, N, rows, width), BF),
            vmem((2, HALF, width), BF),
            vmem((rows, width), F32),
            vmem((rows, width), F32),
            vmem((blocks, rows, width), BF),
            vmem((2, 2, N, QUART, width), BF),
            vmem((2, 2, N, HALF, width), BF),
            vmem((2, 2, QUART, width), BF),
            vmem((2, 2, HALF, width), BF),
            vmem((2, N, HALF, width), BF),
            vmem((N, rows, width), BF),
            vmem((rows, width), BF),
            vmem((rows, width), BF),
            vmem((rows, 128), F32),
            vmem((N, 8, rows), F32),
            vmem((N, 8, rows), F32),
            vmem((N, width, width), F32),
            vmem((N, width, width), BF),
            dma((NSEM,)),
            dma((NSEM,)),
            dma((blocks,)),
            dma((blocks,)),
            dma((2, N)),
            dma((2, N)),
            dma((8,)),
        ],
        compiler_params=pltpu.CompilerParams(
            collective_id=0, has_side_effects=True, vmem_limit_bytes=58 * 1024 * 1024,
        ),
        name="window_grad",
    )(
        states.reshape(rows, width),
        weights.reshape(blocks, width, width),
        head,
        lengths,
        rewards,
    )
    return out.reshape(1, N * width, width)


def solution(mesh):
    placed = (P("role", None, "mp"), P("section", None, "mp"), P("mp"), P("role"), P("role"))
    return jax.shard_map(
        per_device,
        mesh=mesh,
        in_specs=placed,
        out_specs=P("section", "role", "mp"),
        check_vma=False,
    )
```

```python
import functools
import math

import jax
import jax.numpy as jnp
from jax import lax
from jax.experimental import pallas as pl
from jax.experimental.pallas import tpu as pltpu
from jax.sharding import PartitionSpec as P

MESH = pl.DeviceIdType.MESH
BF = jnp.bfloat16
F32 = jnp.float32
GAMMA = 0.97

N = 4
ROWS = 256
BATCH = 128
HALF = 64
QUART = 32
W = 512
NSEM = 300
HALVES = ((0, "x", "z"), (HALF, "z", "x"), (BATCH, "x", "z"), (BATCH + HALF, "z", "x"))
SIGNS = (1, -1)


def sigmoid(v):
    return 1.0 / (1.0 + jnp.exp(-v))


def kernel(states, weight, head_ref, lengths, rewards, out, wv, gath, across, relay, acc, slope,
           part, r1, r2, r3, r4, sums, dz, dzt, y1, err, vx, vz, gacc, gout,
           send_sem, recv_sem, far_send, far_recv, pair_send, pair_recv, local_sem):
    role = lax.axis_index("role")
    section = lax.axis_index("section")
    mp = lax.axis_index("mp")
    pos = {"z": mp // N, "x": mp % N}
    me = {"role": role, "section": section, "mp": mp}

    def slot(**off):
        z = lax.rem(pos["z"] + off.get("z", 0) % N, N)
        x = lax.rem(pos["x"] + off.get("x", 0) % N, N)
        return z * N + x

    def role_at(off):
        return lax.rem(role + off % N, N)

    def device(mp_index=None, role_index=None, sec=None):
        return (
            role if role_index is None else role_index,
            section if sec is None else sec,
            mp if mp_index is None else mp_index,
        )

    numbers = {}

    def number(key):
        return numbers.setdefault(key, len(numbers))

    def move(key, src, dst, dev):
        i = number(key)
        assert i < NSEM
        return pltpu.make_async_remote_copy(
            src_ref=src, dst_ref=dst, send_sem=send_sem.at[i], recv_sem=recv_sem.at[i],
            device_id=dev, device_id_type=MESH,
        )

    started = []

    def send(key, src, dst, dev):
        copy = move(key, src, dst, dev)
        copy.start()
        started.append(copy)

    def arrive(key, dst):
        move(key, dst, dst, device(mp_index=slot(x=1))).wait_recv()

    def drain():
        for copy in started:
            copy.wait_send()
        started.clear()

    def rows_of(base, sign):
        return pl.ds(base + (0 if sign > 0 else QUART), QUART)

    def halves(b):
        return [(h, HALVES[h]) for h in (2 * b, 2 * b + 1)]

    def batch(b):
        return pl.ds(b * BATCH, BATCH)

    def gather_first(src, sec, b):
        for h, _ in halves(b):
            base, f, g = HALVES[h]
            rows = pl.ds(base, HALF)
            for axis, kind in ((f, "f"), (g, "g")):
                for sg in SIGNS:
                    key = ("f", sec, h, sg) if kind == "f" else ("g", sec, h, sg, 0)
                    send(key, src.at[rows], gath.at[mp, rows], device(slot(**{axis: sg}), sec=sec))

    def gather_rest(sec, b, use):
        def region(h, df, dg, rows):
            _, f, g = HALVES[h]
            return gath.at[slot(**{f: df, g: dg}), rows]

        def forward(key, ref, axis, sg):
            send(key, ref, ref, device(slot(**{axis: sg})))

        for sg in SIGNS:
            for h, (base, f, g) in halves(b):
                rows = pl.ds(base, HALF)
                block = region(h, -sg, 0, rows)
                arrive(("f", sec, h, sg), block)
                forward(("o", sec, h, sg), region(h, -sg, 0, rows_of(base, sg)), f, sg)
                for s2 in SIGNS:
                    forward(("g", sec, h, s2, sg), block, g, s2)
        yield
        for sg in SIGNS:
            for h, (base, f, g) in halves(b):
                rows = pl.ds(base, HALF)
                arrive(("g", sec, h, sg, 0), region(h, 0, -sg, rows))
                forward(("t", sec, h, sg, 0), region(h, 0, -sg, rows_of(base, sg)), g, sg)
        yield
        for sg in SIGNS:
            for h, (base, f, g) in halves(b):
                block = region(h, 2, 0, rows_of(base, sg))
                arrive(("o", sec, h, sg), block)
                for s2 in SIGNS:
                    forward(("g", sec, h, s2, 2 * sg), block, g, s2)
        use([(0, 0), (0, 1), (0, -1), (1, 0), (-1, 0)])
        yield
        for sf in SIGNS:
            for sg in SIGNS:
                for h, (base, f, g) in halves(b):
                    arrive(("g", sec, h, sg, sf), region(h, -sf, -sg, pl.ds(base, HALF)))
                    forward(("t", sec, h, sg, sf), region(h, -sf, -sg, rows_of(base, sg)), g, sg)
        yield
        for sg in SIGNS:
            for h, (base, f, g) in halves(b):
                arrive(("g", sec, h, sg, 2 * sg), region(h, 2, -sg, rows_of(base, sg)))
                forward(("t", sec, h, sg, 2), region(h, 2, -sg, rows_of(base, sg)), g, sg)
        use([(1, 1), (1, -1), (-1, 1), (-1, -1)])
        yield
        for sg in SIGNS:
            for h, (base, f, g) in halves(b):
                arrive(("g", sec, h, sg, -2 * sg), region(h, 2, -sg, rows_of(base, -sg)))
                arrive(("t", sec, h, sg, 0), region(h, 0, 2, rows_of(base, sg)))
        use([(2, 0), (0, 2)])
        yield
        for sf in SIGNS:
            for sg in SIGNS:
                for h, (base, f, g) in halves(b):
                    arrive(("t", sec, h, sg, sf), region(h, -sf, 2, rows_of(base, sg)))
        use([(1, 2), (-1, 2), (2, 1), (2, -1)])
        yield
        for sg in SIGNS:
            for h, (base, f, g) in halves(b):
                arrive(("t", sec, h, sg, 2), region(h, 2, 2, rows_of(base, sg)))
        use([(2, 2)])

    def project(offsets, b, far=True):
        across_send(offsets, b, far)
        rows = batch(b)
        for z_off, x_off in offsets:
            s = slot(z=z_off, x=x_off)
            add = jnp.dot(gath[s, rows], wv[s], preferred_element_type=F32)
            if (z_off, x_off) == (0, 0):
                acc[rows] = add
            else:
                acc[rows] += add

    def across_send(offsets, b, far):
        for z_off, x_off in offsets:
            s = slot(z=z_off, x=x_off)
            to = s // N

            @pl.when(to != role if far else lax.rem(to + role, 2) == 1)
            def _():
                pltpu.make_async_remote_copy(
                    src_ref=gath.at[s, batch(b)], dst_ref=across.at[role, lax.rem(s, N), batch(b)],
                    send_sem=far_send.at[b, s], recv_sem=far_recv.at[b, role * N + lax.rem(s, N)],
                    device_id=device(role_index=to), device_id_type=MESH,
                ).start()

    def across_wait(off, b, wait):
        other = role_at(off)
        for j in range(N):
            copy = pltpu.make_async_remote_copy(
                src_ref=across.at[other, j, batch(b)], dst_ref=across.at[other, j, batch(b)],
                send_sem=far_send.at[b, other * N + j], recv_sem=far_recv.at[b, other * N + j],
                device_id=device(role_index=role_at(1)), device_id_type=MESH,
            )
            copy.wait_recv() if wait == "recv" else copy.wait_send()

    line = (("x", pos["x"]), ("z", pos["z"]))

    def pair_first(h):
        far = role_at(2)
        send(("pair", h), gath.at[far * N + line[h][1], batch(h)], relay.at[h],
             device(role_index=far, sec=0))

    def pair_relay():
        for h, (axis, at) in enumerate(line):
            arrive(("pair", h), relay.at[h])
            for off in (2, 1, 3, 0):
                copy = pltpu.make_async_remote_copy(
                    src_ref=relay.at[h], dst_ref=across.at[role_at(2), at, batch(h)],
                    send_sem=pair_send.at[h, off], recv_sem=pair_recv.at[h, at],
                    device_id=device(slot(**{axis: off}), sec=1), device_id_type=MESH,
                )
                copy.start()
                started.append(copy)

    def pair_wait(h):
        for j in range(N):
            block = across.at[role_at(2), j, batch(h)]
            pltpu.make_async_remote_copy(
                src_ref=block, dst_ref=block, send_sem=pair_send.at[h, j], recv_sem=pair_recv.at[h, j],
                device_id=device(sec=0), device_id_type=MESH,
            ).wait_recv()

    def spread_first(src, sec, h):
        rows = batch(h)
        for off in (2, 1, 3):
            send(("d", sec, h, off), src.at[rows], dz.at[role, rows],
                 device(role_index=role_at(off), sec=sec))

    def spread_wait(sec, off, h):
        arrive(("d", sec, h, -off % N), dz.at[role_at(off), batch(h)])

    tn = (((0,), (0,)), ((), ()))

    def grads(off, b):
        src, rows = role_at(off), batch(b)
        for j in range(N):
            left = gath[role * N + j, rows] if off == 0 else across[src, j, rows]
            add = lax.dot_general(left, dz[src, rows], tn, preferred_element_type=F32)
            if (off, b) == (0, 0):
                gacc[j] = add
            elif (off, b) == (2, 1):
                gout[j] = (gacc[j] + add).astype(BF)
                pltpu.make_async_copy(gout.at[j], out.at[j], local_sem.at[2 + j]).start()
            else:
                gacc[j] += add

    def grads_done():
        for j in range(N):
            pltpu.make_async_copy(gout.at[j], out.at[j], local_sem.at[2 + j]).wait()

    def run(steps, count=None):
        for _ in range(100 if count is None else count):
            if next(steps, steps) is steps:
                break

    def by_rows(base, count, body, step=32):
        @pl.loop(0, count // step)
        def _(i):
            body(pl.ds(pl.multiple_of(base + i * step, step), step))

    load_w = pltpu.make_async_copy(weight, wv, local_sem.at[0])
    load_w.start()
    own_copy = pltpu.make_async_copy(states, gath.at[mp], local_sem.at[1])

    @pl.when(section == 0)
    def _():
        own_copy.start()

    barrier = pltpu.get_barrier_semaphore()
    peers = [device(sec=1 - section)]
    for sec in (section, 1 - section):
        peers += [device(slot(**{a: o}), sec=sec) for a in ("x", "z") for o in (1, 2, 3)]
        peers += [device(role_index=role_at(o), sec=sec) for o in (1, 2, 3)]
    for dev in peers:
        pl.semaphore_signal(barrier, inc=1, device_id=dev, device_id_type=MESH)
    pl.semaphore_wait(barrier, len(peers))

    @pl.when(section == 0)
    def _():
        for b in (0, 1):
            gather_first(states, 0, b)
        own_copy.wait()
        load_w.wait()

        def first_layer(b):
            def body(rows):
                z = acc[rows]
                y1[rows] = (gath[mp, rows].astype(F32) + z * sigmoid(z)).astype(BF)
            for h, (base, f, g) in halves(b):
                by_rows(base, HALF, body)
            gather_first(y1, 1, b)
            send(("own", b), y1.at[batch(b)], gath.at[mp, batch(b)], device(sec=1))

        def first_slope(rows):
            z = acc[rows]
            s = sigmoid(z)
            acc[rows] = s * (1.0 + z * (1.0 - s))

        early = gather_rest(0, 0, functools.partial(project, b=0))
        late = gather_rest(0, 1, functools.partial(project, b=1))
        run(early, 3)
        for _ in range(3):
            run(late, 1)
            run(early, 1)
        run(early)
        first_layer(0)
        run(late)
        first_layer(1)
        for b in (0, 1):
            by_rows(b * BATCH, BATCH, first_slope)
            send(("slope", b), acc.at[batch(b)], slope.at[batch(b)], device(sec=1))
        pair_relay()
        for b in (0, 1):
            arrive(("down", b), dz.at[role, batch(b)])
            grads(0, b)
            for off in (1, 3, 2):
                across_wait(off, b, "recv")
                spread_wait(0, off, b)
                grads(off, b)
        grads_done()
        for b in (0, 1):
            for off in (1, 2, 3):
                across_wait(off, b, "send")
        drain()

    @pl.when(section == 1)
    def _():
        load_w.wait()

        def use(offsets, b):
            if (0, 0) in offsets:
                arrive(("own", b), gath.at[mp, batch(b)])
            project(offsets, b, far=False)

        head = head_ref[...].reshape(1, W)
        head_f = head.astype(F32)
        nt = (((1,), (1,)), ((), ()))
        order = (2, 1, 3, 0)

        def second_layer(b):
            def body(rows):
                z = acc[rows]
                s = sigmoid(z)
                y1[rows] = (gath[mp, rows].astype(F32) + z * s).astype(BF)
                g = head_f * (s * (1.0 + z * (1.0 - s)))
                acc[rows] = g
                dzt[rows] = g.astype(BF)
            by_rows(b * BATCH, BATCH, body)

        made = set()

        def make(h, df, dg):
            _, f, g = HALVES[h]
            off = {f: df % N, g: dg % N}
            s, b = slot(**off), h // 2
            key = (b, off["z"], off["x"])
            if key not in made:
                made.add(key)
                rows = batch(b)
                part[s, rows] = lax.dot_general(
                    dzt[rows], wv[s], nt, preferred_element_type=F32).astype(BF)
            return s

        def sum_far(b):
            for dg in order:
                for h, (base, f, g) in halves(b):
                    s = make(h, 2, dg)
                    for k, sg in enumerate(SIGNS):
                        send(("r1", h, sg, dg), part.at[s, rows_of(base, sg)], r1.at[h, k, dg],
                             device(slot(**{f: sg})))
                yield

        def sum_near(b):
            for dg in order:
                for h, (base, f, g) in halves(b):
                    for k, sg in enumerate(SIGNS):
                        s = make(h, sg, dg)
                        arrive(("r1", h, sg, dg), r1.at[h, k, dg])
                        rows = rows_of(base, sg)
                        part[s, rows] = (part[s, rows].astype(F32) + r1[h, k, dg].astype(F32)).astype(BF)
                        send(("r2", h, sg, dg), part.at[s, pl.ds(base, HALF)], r2.at[h, k, dg],
                             device(slot(**{f: sg})))
                yield
            make(2 * b, 0, 0)

        def sum_second(b):
            for dg in order:
                for h, (base, f, g) in halves(b):
                    s = slot(**{f: 0, g: dg})
                    rows = pl.ds(base, HALF)
                    for k, sg in enumerate(SIGNS):
                        arrive(("r2", h, sg, dg), r2.at[h, k, dg])
                    total = part[s, rows].astype(F32) + r2[h, 0, dg].astype(F32) + r2[h, 1, dg].astype(F32)
                    sums[h, dg] = total.astype(BF)
                    if dg == 2:
                        for k, sg in enumerate(SIGNS):
                            send(("r3", h, sg), sums.at[h, dg, rows_of(0, sg)], r3.at[h, k],
                                 device(slot(**{g: sg})))
                    elif dg in (1, 3):
                        sg = 1 if dg == 1 else -1
                        k = SIGNS.index(sg)
                        arrive(("r3", h, sg), r3.at[h, k])
                        rows = rows_of(0, sg)
                        sums[h, dg, rows] = (sums[h, dg, rows].astype(F32) + r3[h, k].astype(F32)).astype(BF)
                        send(("r4", h, sg), sums.at[h, dg], r4.at[h, k], device(slot(**{g: sg})))
                yield

        def finish(b):
            arrive(("slope", b), slope.at[batch(b)])
            for h, (base, f, g) in halves(b):
                for k, sg in enumerate(SIGNS):
                    arrive(("r4", h, sg), r4.at[h, k])

                @pl.loop(0, HALF // 32)
                def _(i):
                    low = pl.ds(pl.multiple_of(i * 32, 32), 32)
                    rows = pl.ds(pl.multiple_of(base + i * 32, 32), 32)
                    back = sums[h, 0, low].astype(F32) + r4[h, 0, low].astype(F32) + r4[h, 1, low].astype(F32)
                    e = err[rows][:, 0:1]
                    dx = (e * head_f + e * back).astype(BF).astype(F32)
                    dzt[rows] = (dx * slope[rows]).astype(BF)
            spread_first(dzt, 0, b)
            send(("down", b), dzt.at[batch(b)], dz.at[role, batch(b)], device(sec=0))

        run(gather_rest(1, 0, functools.partial(use, b=0)))
        pair_first(0)
        second_layer(0)
        far = sum_far(0)
        late = gather_rest(1, 1, functools.partial(use, b=1))
        for _ in range(4):
            run(late, 1)
            run(far, 1)
        run(far)
        run(late)
        pair_first(1)
        second_layer(1)
        vx[0] = lax.dot_general(jnp.broadcast_to(head, (16, W)), y1[...], nt,
                                preferred_element_type=F32)[:8]
        for o in (1, 2, 3):
            send(("vx", o), vx.at[0], vx.at[o], device(slot(x=o)))
        near, far = sum_near(0), sum_far(1)
        for _ in range(4):
            run(near, 1)
            run(far, 1)
        run(near)
        run(far)
        for o in (1, 2, 3):
            arrive(("vx", o), vx.at[o])
        vz[0] = (vx[0] + vx[1]) + (vx[2] + vx[3])
        for o in (1, 2, 3):
            send(("vz", o), vz.at[0], vz.at[o], device(slot(z=o)))
        near, second = sum_near(1), sum_second(0)
        for _ in range(4):
            run(second, 1)
            run(near, 1)
        run(second)
        run(near)

        for o in (1, 2, 3):
            arrive(("vz", o), vz.at[o])
        value = (vz[0] + vz[1]) + (vz[2] + vz[3])
        lane = lax.broadcasted_iota(jnp.int32, (8, ROWS), 1)
        count = lengths.shape[0]
        span = ROWS // count
        place, which = lane % span, lane // span
        length = jnp.full((8, ROWS), lengths[0], jnp.int32)
        reward = jnp.full((8, ROWS), rewards[0], jnp.int32)
        for d in range(1, count):
            length = jnp.where(which == d, lengths[d], length)
            reward = jnp.where(which == d, rewards[d], reward)
        live = place < length
        mask = live.astype(F32)
        power = jnp.where(live, length - 1 - place, 0).astype(F32)
        target = reward.astype(F32) / 1000.0 * jnp.exp(power * math.log(GAMMA)) * mask
        error = (value - target.astype(BF).astype(F32)) * mask
        err[...] = jnp.broadcast_to(error[0:1], (128, ROWS)).T
        finish(0)

        def second_grad(rows):
            dz[role, rows] = (err[rows][:, 0:1] * acc[rows]).astype(BF)
        by_rows(0, ROWS, second_grad)
        for b in (0, 1):
            spread_first(dz.at[role], 1, b)
        run(sum_second(1))
        finish(1)
        for b in (0, 1):
            grads(0, b)
        for off in (1, 3, 2):
            for b in (0, 1):
                spread_wait(1, off, b)
                if off == 2:
                    pair_wait(b)
                else:
                    across_wait(off, b, "recv")
                grads(off, b)
        grads_done()
        for b in (0, 1):
            for off in (1, 3):
                across_wait(off, b, "send")
        drain()


def per_device(states, weights, head, lengths, rewards):
    dialogs, span, width = states.shape
    rows = dialogs * span
    deep = weights.shape[1]
    blocks = deep // width
    dma = pltpu.SemaphoreType.DMA
    vmem = pltpu.VMEM
    out = pl.pallas_call(
        kernel,
        out_shape=jax.ShapeDtypeStruct((N, width, width), BF),
        in_specs=[
            pl.BlockSpec(memory_space=pltpu.HBM),
            pl.BlockSpec(memory_space=pltpu.HBM),
            pl.BlockSpec(memory_space=pltpu.VMEM),
            pl.BlockSpec(memory_space=pltpu.SMEM),
            pl.BlockSpec(memory_space=pltpu.SMEM),
        ],
        out_specs=pl.BlockSpec(memory_space=pl.ANY),
        scratch_shapes=[
            vmem((blocks, width, width), BF),
            vmem((blocks, rows, width), BF),
            vmem((N, N, rows, width), BF),
            vmem((2, BATCH, width), BF),
            vmem((rows, width), F32),
            vmem((rows, width), F32),
            vmem((blocks, rows, width), BF),
            vmem((4, 2, N, QUART, width), BF),
            vmem((4, 2, N, HALF, width), BF),
            vmem((4, 2, QUART, width), BF),
            vmem((4, 2, HALF, width), BF),
            vmem((4, N, HALF, width), BF),
            vmem((N, rows, width), BF),
            vmem((rows, width), BF),
            vmem((rows, width), BF),
            vmem((rows, 128), F32),
            vmem((N, 8, rows), F32),
            vmem((N, 8, rows), F32),
            vmem((N, width, width), F32),
            vmem((N, width, width), BF),
            dma((NSEM,)),
            dma((NSEM,)),
            dma((2, blocks)),
            dma((2, blocks)),
            dma((2, N)),
            dma((2, N)),
            dma((8,)),
        ],
        compiler_params=pltpu.CompilerParams(
            collective_id=0, has_side_effects=True, vmem_limit_bytes=58 * 1024 * 1024,
        ),
        name="window_grad",
    )(
        states.reshape(rows, width),
        weights.reshape(blocks, width, width),
        head,
        lengths,
        rewards,
    )
    return out.reshape(1, N * width, width)


def solution(mesh):
    placed = (P("role", None, "mp"), P("section", None, "mp"), P("mp"), P("role"), P("role"))
    return jax.shard_map(
        per_device,
        mesh=mesh,
        in_specs=placed,
        out_specs=P("section", "role", "mp"),
        check_vma=False,
    )
```

```python
import functools
import math

import jax
import jax.numpy as jnp
from jax import lax
from jax.experimental import pallas as pl
from jax.experimental.pallas import tpu as pltpu
from jax.sharding import PartitionSpec as P

MESH = pl.DeviceIdType.MESH
BF = jnp.bfloat16
F32 = jnp.float32
GAMMA = 0.97

N = 4
ROWS = 256
HALF = 128
QUART = 64
W = 512
NSEM = 200
HALVES = ((0, "x", "z"), (HALF, "z", "x"))
SIGNS = (1, -1)


def sigmoid(v):
    return 1.0 / (1.0 + jnp.exp(-v))


def kernel(states, weight, head_ref, lengths, rewards, out, wv, gath, across, relay, acc, slope,
           part, r1, r2, r3, r4, sums, dz, dzt, y1, err, vx, vz, gacc, gout,
           send_sem, recv_sem, far_send, far_recv, pair_send, pair_recv, local_sem):
    role = lax.axis_index("role")
    section = lax.axis_index("section")
    mp = lax.axis_index("mp")
    pos = {"z": mp // N, "x": mp % N}
    me = {"role": role, "section": section, "mp": mp}

    def slot(**off):
        z = lax.rem(pos["z"] + off.get("z", 0) % N, N)
        x = lax.rem(pos["x"] + off.get("x", 0) % N, N)
        return z * N + x

    def role_at(off):
        return lax.rem(role + off % N, N)

    def device(mp_index=None, role_index=None, sec=None):
        return (
            role if role_index is None else role_index,
            section if sec is None else sec,
            mp if mp_index is None else mp_index,
        )

    numbers = {}

    def number(key):
        return numbers.setdefault(key, len(numbers))

    def move(key, src, dst, dev):
        i = number(key)
        assert i < NSEM
        return pltpu.make_async_remote_copy(
            src_ref=src, dst_ref=dst, send_sem=send_sem.at[i], recv_sem=recv_sem.at[i],
            device_id=dev, device_id_type=MESH,
        )

    started = []

    def send(key, src, dst, dev):
        copy = move(key, src, dst, dev)
        copy.start()
        started.append(copy)

    def arrive(key, dst):
        move(key, dst, dst, device(mp_index=slot(x=1))).wait_recv()

    def drain():
        for copy in started:
            copy.wait_send()
        started.clear()

    def rows_of(base, sign):
        return pl.ds(base + (0 if sign > 0 else QUART), QUART)

    def gather_first(src, sec, halves=(0, 1)):
        for h in halves:
            base, f, g = HALVES[h]
            rows = pl.ds(base, HALF)
            for axis, kind in ((f, "f"), (g, "g")):
                for sg in SIGNS:
                    key = ("f", sec, h, sg) if kind == "f" else ("g", sec, h, sg, 0)
                    send(key, src.at[rows], gath.at[mp, rows], device(slot(**{axis: sg}), sec=sec))

    def gather_rest(sec, use):
        def region(h, df, dg, rows):
            _, f, g = HALVES[h]
            return gath.at[slot(**{f: df, g: dg}), rows]

        def forward(key, ref, axis, sg):
            send(key, ref, ref, device(slot(**{axis: sg})))

        for sg in SIGNS:
            for h, (base, f, g) in enumerate(HALVES):
                rows = pl.ds(base, HALF)
                block = region(h, -sg, 0, rows)
                arrive(("f", sec, h, sg), block)
                forward(("o", sec, h, sg), region(h, -sg, 0, rows_of(base, sg)), f, sg)
                for s2 in SIGNS:
                    forward(("g", sec, h, s2, sg), block, g, s2)
        for sg in SIGNS:
            for h, (base, f, g) in enumerate(HALVES):
                rows = pl.ds(base, HALF)
                arrive(("g", sec, h, sg, 0), region(h, 0, -sg, rows))
                forward(("t", sec, h, sg, 0), region(h, 0, -sg, rows_of(base, sg)), g, sg)
        for sg in SIGNS:
            for h, (base, f, g) in enumerate(HALVES):
                block = region(h, 2, 0, rows_of(base, sg))
                arrive(("o", sec, h, sg), block)
                for s2 in SIGNS:
                    forward(("g", sec, h, s2, 2 * sg), block, g, s2)
        use([(0, 0), (0, 1), (0, -1), (1, 0), (-1, 0)])
        for sf in SIGNS:
            for sg in SIGNS:
                for h, (base, f, g) in enumerate(HALVES):
                    arrive(("g", sec, h, sg, sf), region(h, -sf, -sg, pl.ds(base, HALF)))
                    forward(("t", sec, h, sg, sf), region(h, -sf, -sg, rows_of(base, sg)), g, sg)
        for sg in SIGNS:
            for h, (base, f, g) in enumerate(HALVES):
                arrive(("g", sec, h, sg, 2 * sg), region(h, 2, -sg, rows_of(base, sg)))
                forward(("t", sec, h, sg, 2), region(h, 2, -sg, rows_of(base, sg)), g, sg)
        use([(1, 1), (1, -1), (-1, 1), (-1, -1)])
        for sg in SIGNS:
            for h, (base, f, g) in enumerate(HALVES):
                arrive(("g", sec, h, sg, -2 * sg), region(h, 2, -sg, rows_of(base, -sg)))
                arrive(("t", sec, h, sg, 0), region(h, 0, 2, rows_of(base, sg)))
        use([(2, 0), (0, 2)])
        for sf in SIGNS:
            for sg in SIGNS:
                for h, (base, f, g) in enumerate(HALVES):
                    arrive(("t", sec, h, sg, sf), region(h, -sf, 2, rows_of(base, sg)))
        use([(1, 2), (-1, 2), (2, 1), (2, -1)])
        for sg in SIGNS:
            for h, (base, f, g) in enumerate(HALVES):
                arrive(("t", sec, h, sg, 2), region(h, 2, 2, rows_of(base, sg)))
        use([(2, 2)])

    def project(offsets, far=True):
        across_send(offsets, far)
        for dz_, dx_ in offsets:
            s = slot(z=dz_, x=dx_)
            add = jnp.dot(gath[s], wv[s], preferred_element_type=F32)
            if (dz_, dx_) == (0, 0):
                acc[...] = add
            else:
                acc[...] += add

    def across_send(offsets, far):
        for z_off, x_off in offsets:
            s = slot(z=z_off, x=x_off)
            to = s // N

            @pl.when(to != role if far else lax.rem(to + role, 2) == 1)
            def _():
                pltpu.make_async_remote_copy(
                    src_ref=gath.at[s], dst_ref=across.at[role, lax.rem(s, N)],
                    send_sem=far_send.at[s], recv_sem=far_recv.at[role * N + lax.rem(s, N)],
                    device_id=device(role_index=to), device_id_type=MESH,
                ).start()

    def across_wait(off, wait):
        other = role_at(off)
        for j in range(N):
            copy = pltpu.make_async_remote_copy(
                src_ref=across.at[other, j], dst_ref=across.at[other, j],
                send_sem=far_send.at[other * N + j], recv_sem=far_recv.at[other * N + j],
                device_id=device(role_index=role_at(1)), device_id_type=MESH,
            )
            copy.wait_recv() if wait == "recv" else copy.wait_send()

    line = (("x", pos["x"]), ("z", pos["z"]))

    def pair_first():
        far = role_at(2)
        for h, (axis, at) in enumerate(line):
            send(("pair", h), gath.at[far * N + at, pl.ds(h * HALF, HALF)], relay.at[h],
                 device(role_index=far, sec=0))

    def pair_relay():
        for h, (axis, at) in enumerate(line):
            arrive(("pair", h), relay.at[h])
            for off in (2, 1, 3, 0):
                copy = pltpu.make_async_remote_copy(
                    src_ref=relay.at[h], dst_ref=across.at[role_at(2), at, pl.ds(h * HALF, HALF)],
                    send_sem=pair_send.at[h, off], recv_sem=pair_recv.at[h, at],
                    device_id=device(slot(**{axis: off}), sec=1), device_id_type=MESH,
                )
                copy.start()
                started.append(copy)

    def pair_wait():
        for h in (0, 1):
            for j in range(N):
                block = across.at[role_at(2), j, pl.ds(h * HALF, HALF)]
                pltpu.make_async_remote_copy(
                    src_ref=block, dst_ref=block, send_sem=pair_send.at[h, j], recv_sem=pair_recv.at[h, j],
                    device_id=device(sec=0), device_id_type=MESH,
                ).wait_recv()

    def spread_first(src, sec, h):
        rows = pl.ds(h * HALF, HALF)
        for off in (2, 1, 3):
            send(("d", sec, h, off), src.at[rows], dz.at[role, rows],
                 device(role_index=role_at(off), sec=sec))

    def spread_wait(sec, off):
        for h in (0, 1):
            arrive(("d", sec, h, -off % N), dz.at[role_at(off), pl.ds(h * HALF, HALF)])

    tn = (((0,), (0,)), ((), ()))

    def grads(off):
        src = role_at(off)
        for j in range(N):
            left = gath[role * N + j] if off == 0 else across[src, j]
            add = lax.dot_general(left, dz[src], tn, preferred_element_type=F32)
            if off == 0:
                gacc[j] = add
            elif off == 2:
                gout[j] = (gacc[j] + add).astype(BF)
                pltpu.make_async_copy(gout.at[j], out.at[j], local_sem.at[2 + j]).start()
            else:
                gacc[j] += add

    def grads_done():
        for j in range(N):
            pltpu.make_async_copy(gout.at[j], out.at[j], local_sem.at[2 + j]).wait()

    def by_rows(base, count, body, step=32):
        @pl.loop(0, count // step)
        def _(i):
            body(pl.ds(pl.multiple_of(base + i * step, step), step))

    load_w = pltpu.make_async_copy(weight, wv, local_sem.at[0])
    load_w.start()
    own_copy = pltpu.make_async_copy(states, gath.at[mp], local_sem.at[1])

    @pl.when(section == 0)
    def _():
        own_copy.start()

    barrier = pltpu.get_barrier_semaphore()
    peers = [device(sec=1 - section)]
    for sec in (section, 1 - section):
        peers += [device(slot(**{a: o}), sec=sec) for a in ("x", "z") for o in (1, 2, 3)]
        peers += [device(role_index=role_at(o), sec=sec) for o in (1, 2, 3)]
    for dev in peers:
        pl.semaphore_signal(barrier, inc=1, device_id=dev, device_id_type=MESH)
    pl.semaphore_wait(barrier, len(peers))

    @pl.when(section == 0)
    def _():
        gather_first(states, 0)
        own_copy.wait()
        load_w.wait()
        gather_rest(0, project)
        for h in (0, 1):
            def first_layer(rows):
                z = acc[rows]
                y1[rows] = (gath[mp, rows].astype(F32) + z * sigmoid(z)).astype(BF)
            by_rows(h * HALF, HALF, first_layer)
            gather_first(y1, 1, (h,))
        send(("own",), y1, gath.at[mp], device(sec=1))

        def first_slope(rows):
            z = acc[rows]
            s = sigmoid(z)
            acc[rows] = s * (1.0 + z * (1.0 - s))
        by_rows(0, ROWS, first_slope)
        send(("slope",), acc, slope, device(sec=1))
        pair_relay()
        for h in (0, 1):
            arrive(("down", h), dz.at[role, pl.ds(h * HALF, HALF)])
        grads(0)
        for off in (1, 3, 2):
            spread_wait(0, off)
            across_wait(off, "recv")
            grads(off)
        grads_done()
        for off in (1, 2, 3):
            across_wait(off, "send")
        drain()

    @pl.when(section == 1)
    def _():
        load_w.wait()

        def use(offsets):
            if (0, 0) in offsets:
                arrive(("own",), gath.at[mp])
            project(offsets, far=False)

        gather_rest(1, use)
        pair_first()

        head = head_ref[...].reshape(1, W)
        head_f = head.astype(F32)

        def second_layer(rows):
            z = acc[rows]
            s = sigmoid(z)
            y1[rows] = (gath[mp, rows].astype(F32) + z * s).astype(BF)
            g = head_f * (s * (1.0 + z * (1.0 - s)))
            acc[rows] = g
            dzt[rows] = g.astype(BF)
        by_rows(0, ROWS, second_layer)

        nt = (((1,), (1,)), ((), ()))
        vx[0] = lax.dot_general(jnp.broadcast_to(head, (16, W)), y1[...], nt,
                                preferred_element_type=F32)[:8]
        for o in (1, 2, 3):
            send(("vx", o), vx.at[0], vx.at[o], device(slot(x=o)))

        made = set()

        def make(z_off, x_off):
            z_off, x_off = z_off % N, x_off % N
            if (z_off, x_off) in made:
                return
            made.add((z_off, x_off))
            s = slot(z=z_off, x=x_off)
            part[s] = lax.dot_general(dzt[...], wv[s], nt, preferred_element_type=F32).astype(BF)

        def make_at(h, df, dg):
            _, f, g = HALVES[h]
            off = {f: df, g: dg}
            make(off["z"], off["x"])
            return slot(**off)

        order = (2, 1, 3, 0)
        for dg in order:
            for h, (base, f, g) in enumerate(HALVES):
                s = make_at(h, 2, dg)
                for k, sg in enumerate(SIGNS):
                    send(("r1", h, sg, dg), part.at[s, rows_of(base, sg)], r1.at[h, k, dg],
                         device(slot(**{f: sg})))
        for o in (1, 2, 3):
            arrive(("vx", o), vx.at[o])
        vz[0] = (vx[0] + vx[1]) + (vx[2] + vx[3])
        for o in (1, 2, 3):
            send(("vz", o), vz.at[0], vz.at[o], device(slot(z=o)))
        def value_grad():
            for o in (1, 2, 3):
                arrive(("vz", o), vz.at[o])
            value = (vz[0] + vz[1]) + (vz[2] + vz[3])
            lane = lax.broadcasted_iota(jnp.int32, (8, ROWS), 1)
            count = lengths.shape[0]
            span = ROWS // count
            place, which = lane % span, lane // span
            length = jnp.full((8, ROWS), lengths[0], jnp.int32)
            reward = jnp.full((8, ROWS), rewards[0], jnp.int32)
            for d in range(1, count):
                length = jnp.where(which == d, lengths[d], length)
                reward = jnp.where(which == d, rewards[d], reward)
            live = place < length
            mask = live.astype(F32)
            power = jnp.where(live, length - 1 - place, 0).astype(F32)
            target = reward.astype(F32) / 1000.0 * jnp.exp(power * math.log(GAMMA)) * mask
            error = (value - target.astype(BF).astype(F32)) * mask
            err[...] = jnp.broadcast_to(error[0:1], (128, ROWS)).T

            def second_grad(rows):
                dz[role, rows] = (err[rows][:, 0:1] * acc[rows]).astype(BF)
            by_rows(0, ROWS, second_grad)
            for h in (0, 1):
                spread_first(dz.at[role], 1, h)

        for dg in order:
            for h, (base, f, g) in enumerate(HALVES):
                for k, sg in enumerate(SIGNS):
                    s = make_at(h, sg, dg)
                    arrive(("r1", h, sg, dg), r1.at[h, k, dg])
                    rows = rows_of(base, sg)
                    part[s, rows] = (part[s, rows].astype(F32) + r1[h, k, dg].astype(F32)).astype(BF)
                    send(("r2", h, sg, dg), part.at[s, pl.ds(base, HALF)], r2.at[h, k, dg],
                         device(slot(**{f: sg})))
            if dg == 1:
                value_grad()
        make(0, 0)

        for dg in order:
            for h, (base, f, g) in enumerate(HALVES):
                s = slot(**{f: 0, g: dg})
                rows = pl.ds(base, HALF)
                for k, sg in enumerate(SIGNS):
                    arrive(("r2", h, sg, dg), r2.at[h, k, dg])
                total = part[s, rows].astype(F32) + r2[h, 0, dg].astype(F32) + r2[h, 1, dg].astype(F32)
                sums[h, dg] = total.astype(BF)
                if dg == 2:
                    for k, sg in enumerate(SIGNS):
                        send(("r3", h, sg), sums.at[h, dg, rows_of(0, sg)], r3.at[h, k],
                             device(slot(**{g: sg})))
                elif dg in (1, 3):
                    sg = 1 if dg == 1 else -1
                    k = SIGNS.index(sg)
                    arrive(("r3", h, sg), r3.at[h, k])
                    rows = rows_of(0, sg)
                    sums[h, dg, rows] = (sums[h, dg, rows].astype(F32) + r3[h, k].astype(F32)).astype(BF)
                    send(("r4", h, sg), sums.at[h, dg], r4.at[h, k], device(slot(**{g: sg})))
        arrive(("slope",), slope)
        for h, (base, f, g) in enumerate(HALVES):
            for k, sg in enumerate(SIGNS):
                arrive(("r4", h, sg), r4.at[h, k])

            @pl.loop(0, HALF // 32)
            def _(i):
                low = pl.ds(pl.multiple_of(i * 32, 32), 32)
                rows = pl.ds(pl.multiple_of(base + i * 32, 32), 32)
                back = sums[h, 0, low].astype(F32) + r4[h, 0, low].astype(F32) + r4[h, 1, low].astype(F32)
                e = err[rows][:, 0:1]
                dx = (e * head_f + e * back).astype(BF).astype(F32)
                dzt[rows] = (dx * slope[rows]).astype(BF)
            send(("down", h), dzt.at[pl.ds(base, HALF)], dz.at[role, pl.ds(base, HALF)], device(sec=0))
            spread_first(dzt, 0, h)
        grads(0)
        for off in (1, 3, 2):
            spread_wait(1, off)
            if off == 2:
                pair_wait()
            else:
                across_wait(off, "recv")
            grads(off)
        grads_done()
        for off in (1, 3):
            across_wait(off, "send")
        drain()


def per_device(states, weights, head, lengths, rewards):
    dialogs, span, width = states.shape
    rows = dialogs * span
    deep = weights.shape[1]
    blocks = deep // width
    dma = pltpu.SemaphoreType.DMA
    vmem = pltpu.VMEM
    out = pl.pallas_call(
        kernel,
        out_shape=jax.ShapeDtypeStruct((N, width, width), BF),
        in_specs=[
            pl.BlockSpec(memory_space=pltpu.HBM),
            pl.BlockSpec(memory_space=pltpu.HBM),
            pl.BlockSpec(memory_space=pltpu.VMEM),
            pl.BlockSpec(memory_space=pltpu.SMEM),
            pl.BlockSpec(memory_space=pltpu.SMEM),
        ],
        out_specs=pl.BlockSpec(memory_space=pl.ANY),
        scratch_shapes=[
            vmem((blocks, width, width), BF),
            vmem((blocks, rows, width), BF),
            vmem((N, N, rows, width), BF),
            vmem((2, HALF, width), BF),
            vmem((rows, width), F32),
            vmem((rows, width), F32),
            vmem((blocks, rows, width), BF),
            vmem((2, 2, N, QUART, width), BF),
            vmem((2, 2, N, HALF, width), BF),
            vmem((2, 2, QUART, width), BF),
            vmem((2, 2, HALF, width), BF),
            vmem((2, N, HALF, width), BF),
            vmem((N, rows, width), BF),
            vmem((rows, width), BF),
            vmem((rows, width), BF),
            vmem((rows, 128), F32),
            vmem((N, 8, rows), F32),
            vmem((N, 8, rows), F32),
            vmem((N, width, width), F32),
            vmem((N, width, width), BF),
            dma((NSEM,)),
            dma((NSEM,)),
            dma((blocks,)),
            dma((blocks,)),
            dma((2, N)),
            dma((2, N)),
            dma((8,)),
        ],
        compiler_params=pltpu.CompilerParams(
            collective_id=0, has_side_effects=True, vmem_limit_bytes=58 * 1024 * 1024,
        ),
        name="window_grad",
    )(
        states.reshape(rows, width),
        weights.reshape(blocks, width, width),
        head,
        lengths,
        rewards,
    )
    return out.reshape(1, N * width, width)


def solution(mesh):
    placed = (P("role", None, "mp"), P("section", None, "mp"), P("mp"), P("role"), P("role"))
    return jax.shard_map(
        per_device,
        mesh=mesh,
        in_specs=placed,
        out_specs=P("section", "role", "mp"),
        check_vma=False,
    )
```
